32 devices in a mesh: grp: 2 (over y), res: 4 (over z), br: 2 (over core), aux: 2 (over x).
Axes of the slice: x: 2, y: 2, z: 4, core: 2. Of those that a mesh axis runs over, the one named last changes fastest.
Arguments:
- homolog_features: bfloat16 [32, 128, 256], P(('grp', 'br', 'aux'), 'res'), parts along dimension 0, may hold values from -6 to 6
- couple_features: bfloat16 [256, 128, 128], P(('grp', 'res'), ('br', 'aux')), parts along dimension 0, may hold values from -6 to 6
- symbol_ids: int32 [32, 128], P(('grp', 'br', 'aux'), 'res'), parts along dimension 0, may hold values from 0 to 22
- entry_present: int32 [32, 128], P(('grp', 'br', 'aux'), 'res'), parts along dimension 0, may hold values 0 or 1
- amino_present: int32 [256], P('grp'), parts along dimension 0, may hold values 0 or 1
- symbol_lookup_matrix: bfloat16 [23, 256], replicated, may hold values from -3 to 3
- horizontal_entry_matrix: bfloat16 [256, 1024], replicated, may hold values from -0.375 to 0.375
- couple_logit_matrix: bfloat16 [128, 8], replicated, may hold values from -40 to 40, as said below
- horizontal_exit_matrix: bfloat16 [256, 256], replicated, may hold values from -0.375 to 0.375
- vertical_entry_matrix: bfloat16 [256, 1024], replicated, may hold values from -0.375 to 0.375
- vertical_exit_matrix: bfloat16 [256, 256], replicated, may hold values from -0.375 to 0.375
- feedforward_first_matrix: bfloat16 [256, 1024], replicated, may hold values from -0.375 to 0.375
- feedforward_second_matrix: bfloat16 [1024, 256], replicated, may hold values from -0.1875 to 0.1875
- trimul_entry_matrix: bfloat16 [128, 640], replicated, may hold values from -0.5 to 0.5
- trimul_exit_matrix: bfloat16 [128, 128], replicated, may hold values from -0.5 to 0.5
Outputs:
- alignment_output: bfloat16 [32, 128, 256], P(('grp', 'br', 'aux'), 'res'), parts along dimension 0
- pair_output: bfloat16 [256, 128, 128], P(('grp', 'res'), ('br', 'aux')), parts along dimension 0
The draws below stay inside these ranges and needn't reach their ends.
There are 2 independent parts, one for each index of `grp`. The reference program is written for one: setup_inputs(seed, part) draws one part's arguments, and reference() takes and returns one part's arrays. A program takes and returns all parts, laid end to end along the dimension named above; an argument that names none is the same for every part. Nothing has to cross between parts.
Inputs may be any that keep to these rules, and one draw needn't show every extreme that they name: `couple_logit_matrix`: a projection of the 128 pair channels onto the 8 heads.
All inputs are finite; a program needn't handle non-finite values. No bound on the sum of `entry_present` on one device may be relied on, other than what follows from the above.
Results may differ from the reference program's by a relative error of at most 0.008.
Values may be sent and summed in bfloat16 or wider, within the bound.
A program may use at most 64 MiB of HBM per device.

```python
import jax
import jax.numpy as jnp
from jax import lax

FEATURE_DEPTH = 256
CZ = 128
FOCI_TOTAL = 8
ATTEND_SPAN = 32
SYMBOL_KINDS = 23
HOMOLOG_TOTAL = 16
AMINO_TOTAL = 128
WIDENED_LAYER = 1024


def draw_couple_logit_matrix(key, part):
    base = jax.random.normal(jax.random.fold_in(key, 11), (CZ, FOCI_TOTAL), jnp.float32) * CZ ** (-0.5)
    return base.astype(jnp.bfloat16)


def plant(values, key, low, top_value):
    shape = values.shape
    spot = [jax.random.randint(jax.random.fold_in(key, axis), (), 0, shape[axis]) for axis in range(len(shape))]
    values = values.at[tuple(spot)].set(low)
    longest = shape.index(max(shape))
    spot[longest] = (spot[longest] + 1) % shape[longest]
    return values.at[tuple(spot)].set(top_value)


def level_of(own_key, dims, split, least, largest):
    def one(dim, parts):
        draws = jax.random.uniform(jax.random.fold_in(jax.random.fold_in(own_key, 6), dim), (parts,), jnp.float32, least / len(split), largest / len(split))
        return jnp.repeat(jnp.exp(draws), dims[dim] // parts).reshape((-1,) + (1,) * (len(dims) - dim - 1))

    level = one(*split[0])
    for cut in split[1:]:
        level = level * one(*cut)
    return level


def gaussian(key, extent, spread, reach, pieces=(), kind=jnp.bfloat16):
    array = jax.random.normal(key, extent, jnp.float32) * spread
    if len(pieces) > 0:
        array = level_of(key, extent, pieces, -0.22, 0.18) * array
    return jnp.clip(array, min=-reach, max=reach).astype(kind)


def setup_inputs(seed: int = 0, part: int = 0) -> dict:
    key_list = jax.random.split(jax.random.key(seed), 16)
    own_keys = jax.random.split(jax.random.fold_in(key_list[15], part), 16)
    homolog_features = gaussian(own_keys[0], (HOMOLOG_TOTAL, AMINO_TOTAL, FEATURE_DEPTH), 1.0, 6.0, ((0, 4), (1, 4)))
    couple_features = gaussian(own_keys[1], (AMINO_TOTAL, AMINO_TOTAL, CZ), 1.0, 6.0, ((0, 4), (1, 4)))
    symbol_ids = plant(jax.random.randint(own_keys[2], (HOMOLOG_TOTAL, AMINO_TOTAL), 0, SYMBOL_KINDS), jax.random.fold_in(own_keys[2], 1), 0, SYMBOL_KINDS - 1).astype(jnp.int32)
    entry_present = plant((jax.random.randint(own_keys[3], (HOMOLOG_TOTAL, AMINO_TOTAL), 0, 4) < 3).astype(jnp.int32), jax.random.fold_in(own_keys[3], 1), 0, 1)
    amino_present = plant((jax.random.randint(own_keys[4], (AMINO_TOTAL,), 0, 8) < 7).astype(jnp.int32), jax.random.fold_in(own_keys[4], 1), 0, 1)
    symbol_lookup_matrix = gaussian(key_list[5], (SYMBOL_KINDS, FEATURE_DEPTH), 0.5, 3.0)
    horizontal_entry_matrix = gaussian(key_list[6], (FEATURE_DEPTH, 4 * FEATURE_DEPTH), FEATURE_DEPTH ** -0.5, 0.375)
    couple_logit_matrix = draw_couple_logit_matrix(jax.random.fold_in(key_list[15], 71), part)
    horizontal_exit_matrix = gaussian(key_list[8], (FEATURE_DEPTH, FEATURE_DEPTH), FEATURE_DEPTH ** -0.5, 0.375)
    vertical_entry_matrix = gaussian(key_list[9], (FEATURE_DEPTH, 4 * FEATURE_DEPTH), FEATURE_DEPTH ** -0.5, 0.375)
    vertical_exit_matrix = gaussian(key_list[10], (FEATURE_DEPTH, FEATURE_DEPTH), FEATURE_DEPTH ** -0.5, 0.375)
    feedforward_first_matrix = gaussian(key_list[11], (FEATURE_DEPTH, WIDENED_LAYER), FEATURE_DEPTH ** -0.5, 0.375)
    feedforward_second_matrix = gaussian(key_list[12], (WIDENED_LAYER, FEATURE_DEPTH), WIDENED_LAYER ** -0.5, 0.1875)
    trimul_entry_matrix = gaussian(key_list[13], (CZ, 5 * CZ), CZ ** -0.5, 0.5)
    trimul_exit_matrix = gaussian(key_list[14], (CZ, CZ), CZ ** -0.5, 0.5)
    return dict(homolog_features=homolog_features, couple_features=couple_features, symbol_ids=symbol_ids, entry_present=entry_present, amino_present=amino_present, symbol_lookup_matrix=symbol_lookup_matrix, horizontal_entry_matrix=horizontal_entry_matrix, couple_logit_matrix=couple_logit_matrix, horizontal_exit_matrix=horizontal_exit_matrix, vertical_entry_matrix=vertical_entry_matrix, vertical_exit_matrix=vertical_exit_matrix, feedforward_first_matrix=feedforward_first_matrix, feedforward_second_matrix=feedforward_second_matrix, trimul_entry_matrix=trimul_entry_matrix, trimul_exit_matrix=trimul_exit_matrix)


epsilon = 1e-05
masked_fill_value = 1000000000.0

def normalize(inputs):
    values = inputs.astype(jnp.float32)
    average = lax.optimization_barrier(jnp.mean(values, axis=-1, keepdims=True))
    centred = values - average
    variance = lax.optimization_barrier(jnp.mean(centred * centred, axis=-1, keepdims=True))
    return centred * lax.rsqrt(variance + epsilon)

def apply_projection(row_block, weight):
    flattened = row_block.reshape(-1, row_block.shape[-1])
    result = jnp.dot(flattened, weight, preferred_element_type=jnp.float32)
    return result.reshape(row_block.shape[:-1] + (weight.shape[1],))

def attend(queries, key_rows, value_rows, bias_block, penalty):
    scores = jnp.einsum('qhd,khd->hqk', queries.astype(jnp.float32), key_rows.astype(jnp.float32)) * ATTEND_SPAN ** (-0.5)
    scores = scores + bias_block + penalty
    row_max = lax.optimization_barrier(jnp.max(scores, axis=-1, keepdims=True))
    powers = jnp.exp(scores - row_max)
    weights = (powers / lax.optimization_barrier(jnp.sum(powers, axis=-1, keepdims=True))).astype(jnp.bfloat16)
    return jnp.einsum('hqk,khd->qhd', weights.astype(jnp.float32), value_rows.astype(jnp.float32))

def reference(homolog_features, couple_features, symbol_ids, entry_present, amino_present, symbol_lookup_matrix, horizontal_entry_matrix, couple_logit_matrix, horizontal_exit_matrix, vertical_entry_matrix, vertical_exit_matrix, feedforward_first_matrix, feedforward_second_matrix, trimul_entry_matrix, trimul_exit_matrix):
    indicator_symbols = (symbol_ids[..., None] == jnp.arange(SYMBOL_KINDS, dtype=jnp.int32)[None, None, :]).astype(jnp.float32)
    symbol_vectors = homolog_features.astype(jnp.float32) + jnp.einsum('zas,sv->zav', indicator_symbols, symbol_lookup_matrix.astype(jnp.float32))
    normed_first = normalize(symbol_vectors).astype(jnp.bfloat16)
    horizontal_combined = apply_projection(normed_first, horizontal_entry_matrix)
    horizontal_queries = horizontal_combined[..., :FEATURE_DEPTH].astype(jnp.bfloat16).reshape(HOMOLOG_TOTAL, AMINO_TOTAL, FOCI_TOTAL, ATTEND_SPAN)
    horizontal_keyset = horizontal_combined[..., FEATURE_DEPTH:2 * FEATURE_DEPTH].astype(jnp.bfloat16).reshape(HOMOLOG_TOTAL, AMINO_TOTAL, FOCI_TOTAL, ATTEND_SPAN)
    horizontal_payload = horizontal_combined[..., 2 * FEATURE_DEPTH:3 * FEATURE_DEPTH].astype(jnp.bfloat16).reshape(HOMOLOG_TOTAL, AMINO_TOTAL, FOCI_TOTAL, ATTEND_SPAN)
    horizontal_sigmoid = jax.nn.sigmoid(horizontal_combined[..., 3 * FEATURE_DEPTH:])
    pair_norm = normalize(couple_features).astype(jnp.bfloat16)
    pair_bias = apply_projection(pair_norm, couple_logit_matrix).transpose(2, 0, 1)
    key_mask_penalty = masked_fill_value * (entry_present.astype(jnp.float32) - 1.0)

    def one_row(items):
        queries, key_rows, value_rows, penalty = items
        return attend(queries, key_rows, value_rows, pair_bias, penalty[None, None, :])
    horizontal_context = lax.map(one_row, (horizontal_queries, horizontal_keyset, horizontal_payload, key_mask_penalty))
    horizontal_result = (horizontal_sigmoid * horizontal_context.reshape(HOMOLOG_TOTAL, AMINO_TOTAL, FEATURE_DEPTH)).astype(jnp.bfloat16)
    after_row = symbol_vectors + apply_projection(horizontal_result, horizontal_exit_matrix)
    normed_second = normalize(after_row).astype(jnp.bfloat16)
    vertical_combined = apply_projection(normed_second, vertical_entry_matrix)
    vertical_queries = vertical_combined[..., :FEATURE_DEPTH].astype(jnp.bfloat16).reshape(HOMOLOG_TOTAL, AMINO_TOTAL, FOCI_TOTAL, ATTEND_SPAN)
    vertical_keyset = vertical_combined[..., FEATURE_DEPTH:2 * FEATURE_DEPTH].astype(jnp.bfloat16).reshape(HOMOLOG_TOTAL, AMINO_TOTAL, FOCI_TOTAL, ATTEND_SPAN)
    vertical_payload = vertical_combined[..., 2 * FEATURE_DEPTH:3 * FEATURE_DEPTH].astype(jnp.bfloat16).reshape(HOMOLOG_TOTAL, AMINO_TOTAL, FOCI_TOTAL, ATTEND_SPAN)
    vertical_sigmoid = jax.nn.sigmoid(vertical_combined[..., 3 * FEATURE_DEPTH:])

    def one_column(items):
        queries, key_rows, value_rows, penalty = items
        return attend(queries, key_rows, value_rows, jnp.zeros((1, 1, 1), jnp.float32), penalty[None, None, :])
    vertical_context = lax.map(one_column, (vertical_queries.transpose(1, 0, 2, 3), vertical_keyset.transpose(1, 0, 2, 3), vertical_payload.transpose(1, 0, 2, 3), key_mask_penalty.T))
    vertical_result = (vertical_sigmoid * vertical_context.transpose(1, 0, 2, 3).reshape(HOMOLOG_TOTAL, AMINO_TOTAL, FEATURE_DEPTH)).astype(jnp.bfloat16)
    after_column_update = after_row + apply_projection(vertical_result, vertical_exit_matrix)
    normed_third = normalize(after_column_update).astype(jnp.bfloat16)
    hidden_units = jax.nn.relu(apply_projection(normed_third, feedforward_first_matrix)).astype(jnp.bfloat16)
    alignment_output = (after_column_update + apply_projection(hidden_units, feedforward_second_matrix)).astype(jnp.bfloat16)
    tri_all = apply_projection(pair_norm, trimul_entry_matrix)
    valid_res = amino_present.astype(jnp.float32)
    pair_valid = (valid_res[:, None] * valid_res[None, :])[..., None]
    left_side = (jax.nn.sigmoid(tri_all[..., CZ:2 * CZ]) * tri_all[..., :CZ] * pair_valid).astype(jnp.bfloat16)
    right_side = (jax.nn.sigmoid(tri_all[..., 3 * CZ:4 * CZ]) * tri_all[..., 2 * CZ:3 * CZ] * pair_valid).astype(jnp.bfloat16)
    out_gate = jax.nn.sigmoid(tri_all[..., 4 * CZ:])
    product = jnp.einsum('kic,kjc->ijc', left_side.astype(jnp.float32), right_side.astype(jnp.float32)).astype(jnp.bfloat16)
    normed_final = normalize(product).astype(jnp.bfloat16)
    pair_output = (couple_features.astype(jnp.float32) + out_gate * apply_projection(normed_final, trimul_exit_matrix)).astype(jnp.bfloat16)
    return (alignment_output, pair_output)
```

```python
import functools

import jax
import jax.numpy as jnp
from jax import lax
from jax.experimental import pallas as pl
from jax.experimental.pallas import tpu as pltpu
from jax.sharding import PartitionSpec as P

epsilon = 1e-05
masked_fill_value = 1000000000.0
MESH = pl.DeviceIdType.MESH
f32 = jnp.float32
bf16 = jnp.bfloat16


def normalize(inputs, axis=-1):
    values = inputs.astype(f32)
    average = jnp.mean(values, axis=axis, keepdims=True)
    centred = values - average
    variance = jnp.mean(centred * centred, axis=axis, keepdims=True)
    return centred * lax.rsqrt(variance + epsilon)


def dot(a, b, contract):
    return lax.dot_general(a, b, (contract, ((), ())), preferred_element_type=f32)


class Peers:
    def __init__(self, sizes):
        self.R, self.BR, self.AX = sizes
        self.r = lax.axis_index("res")
        self.b = lax.axis_index("br")
        self.x = lax.axis_index("aux")

    def res(self, d):
        return lax.rem(self.r + d, self.R)

    def br(self, d):
        return lax.rem(self.b + d, self.BR)

    def aux(self, d):
        return lax.rem(self.x + d, self.AX)

    def res_back(self, d):
        return lax.rem(self.r + self.R - d, self.R)

    def aux_back(self, d):
        return lax.rem(self.x + self.AX - d, self.AX)

    def group(self):
        return [(bo, a) for bo in range(self.BR) for a in range(self.AX) if (bo, a) != (0, 0)]

    def barrier(self):
        semaphore = pltpu.get_barrier_semaphore()
        for d in range(1, self.R):
            pl.semaphore_signal(semaphore, inc=1, device_id={"res": self.res(d)}, device_id_type=MESH)
        for bo, a in self.group():
            pl.semaphore_signal(
                semaphore, inc=1, device_id={"br": self.br(bo), "aux": self.aux(a)}, device_id_type=MESH
            )
        pl.semaphore_wait(semaphore, self.R - 1 + self.BR * self.AX - 1)


def remote(src, dst, send, recv, device):
    copy = pltpu.make_async_remote_copy(
        src_ref=src, dst_ref=dst, send_sem=send, recv_sem=recv, device_id=device, device_id_type=MESH
    )
    copy.start()
    return copy


def first_kernel(
    sizes, rows, valid, bias, left, right,
    rows_out, row_valid, bias_out, col_valid, left_out, right_out,
    res_send, res_recv, grp_send, grp_recv, aux_send, aux_recv, br_send, br_recv,
):
    p = Peers(sizes)
    R, BR, AX = sizes
    p.barrier()
    sent = []
    arriving = []
    lefts = {}

    def relay(d, a):
        origin = (p.b, p.aux_back(a), p.res_back(d))
        src = left.at[p.r] if (d, a) == (0, 0) else left_out.at[origin]
        for bo in range(1, BR):
            copy = remote(
                src, left_out.at[origin], br_send.at[d, a, bo], br_recv.at[d, a, bo], {"br": p.br(bo)}
            )
            sent.append(copy)
            arriving.append(copy)

    def spread(d):
        origin = (p.b, p.x, p.res_back(d))
        src = left.at[p.r] if d == 0 else left_out.at[origin]
        copies = {}
        for a in range(1, AX):
            copy = remote(
                src, left_out.at[origin], aux_send.at[d, a], aux_recv.at[d, a], {"aux": p.aux(a)}
            )
            sent.append(copy)
            copies[a] = copy
        relay(d, 0)
        return copies

    for d in range(1, R):
        to = p.res(d)
        lefts[d] = remote(
            left.at[to], left_out.at[p.b, p.x, p.r], res_send.at[0, d], res_recv.at[0, d], {"res": to}
        )
        sent.append(lefts[d])
    spreads = {0: spread(0)}
    for d in range(1, R):
        to = {"res": p.res(d)}
        for n, (src, dst) in enumerate(
            ((rows, rows_out.at[p.r]), (valid, row_valid.at[p.r]), (right.at[p.res(d)], right_out.at[p.r]))
        ):
            copy = remote(src, dst, res_send.at[n + 1, d], res_recv.at[n + 1, d], to)
            sent.append(copy)
            arriving.append(copy)
    for n, (bo, a) in enumerate(p.group()):
        to = {"br": p.br(bo), "aux": p.aux(a)}
        for m, (src, dst) in enumerate(((bias, bias_out), (valid, col_valid))):
            copy = remote(src, dst.at[p.b, p.x], grp_send.at[m, n], grp_recv.at[m, n], to)
            sent.append(copy)
            arriving.append(copy)
    rows_out[p.r] = rows[...]
    row_valid[p.r] = valid[...]
    bias_out[p.b, p.x] = bias[...]
    col_valid[p.b, p.x] = valid[...]
    left_out[p.b, p.x, p.r] = left[p.r]
    right_out[p.r] = right[p.r]
    for d in range(1, R):
        lefts[d].wait_recv()
        spreads[d] = spread(d)
    for d in range(R):
        for a in range(1, AX):
            spreads[d][a].wait_recv()
            relay(d, a)
    for copy in arriving:
        copy.wait_recv()
    for copy in sent:
        copy.wait_send()


def second_kernel(
    sizes, keys, product, keys_out, product_out, res_send, res_recv, aux_send, aux_recv, br_send, br_recv
):
    p = Peers(sizes)
    R, BR, AX = sizes
    p.barrier()
    sent = []
    arriving = []

    def relay(a):
        origin = (p.b, p.aux_back(a))
        src = keys if a == 0 else keys_out.at[origin]
        for bo in range(1, BR):
            copy = remote(src, keys_out.at[origin], br_send.at[a, bo], br_recv.at[a, bo], {"br": p.br(bo)})
            sent.append(copy)
            arriving.append(copy)

    across = {}
    for a in range(1, AX):
        across[a] = remote(
            keys, keys_out.at[p.b, p.x], aux_send.at[a], aux_recv.at[a], {"aux": p.aux(a)}
        )
        sent.append(across[a])
    relay(0)
    for d in range(1, R):
        to = p.res(d)
        copy = remote(product.at[to], product_out.at[p.r], res_send.at[d], res_recv.at[d], {"res": to})
        sent.append(copy)
        arriving.append(copy)
    keys_out[p.b, p.x] = keys[...]
    product_out[p.r] = product[p.r]
    for a in range(1, AX):
        across[a].wait_recv()
        relay(a)
    for copy in arriving:
        copy.wait_recv()
    for copy in sent:
        copy.wait_send()


def call(body, name, collective, shapes, semaphores, operands):
    vmem = pl.BlockSpec(memory_space=pltpu.VMEM)
    return pl.pallas_call(
        body,
        name=name,
        out_shape=[jax.ShapeDtypeStruct(*shape) for shape in shapes],
        in_specs=[vmem] * len(operands),
        out_specs=[vmem] * len(shapes),
        scratch_shapes=[pltpu.SemaphoreType.DMA(shape) for shape in semaphores],
        compiler_params=pltpu.CompilerParams(collective_id=collective, has_side_effects=True),
    )(*operands)


def attention_row(queries, keys, values, bias, penalty, scale):
    scores = jnp.einsum("sihd,sjhd->shij", queries, keys, preferred_element_type=f32) * scale
    scores = scores + bias[None] + penalty[:, None, None, :]
    powers = jnp.exp(scores - jnp.max(scores, axis=-1, keepdims=True))
    total = jnp.sum(powers, axis=-1)
    mixed = jnp.einsum("shij,sjhd->sihd", powers.astype(bf16), values, preferred_element_type=f32)
    return mixed / jnp.transpose(total, (0, 2, 1))[..., None]


def attention_column(queries, keys, values, penalty, scale):
    scores = jnp.einsum("srhd,trhd->rhst", queries, keys, preferred_element_type=f32) * scale
    scores = scores + penalty.T[:, None, None, :]
    powers = jnp.exp(scores - jnp.max(scores, axis=-1, keepdims=True))
    total = jnp.sum(powers, axis=-1)
    mixed = jnp.einsum("rhst,trhd->srhd", powers.astype(bf16), values, preferred_element_type=f32)
    return mixed / jnp.transpose(total, (2, 0, 1))[..., None]


def on_device(
    sizes,
    homolog_features,
    couple_features,
    symbol_ids,
    entry_present,
    amino_present,
    symbol_lookup_matrix,
    horizontal_entry_matrix,
    couple_logit_matrix,
    horizontal_exit_matrix,
    vertical_entry_matrix,
    vertical_exit_matrix,
    feedforward_first_matrix,
    feedforward_second_matrix,
    trimul_entry_matrix,
    trimul_exit_matrix,
):
    R, BR, AX = sizes
    B = BR * AX
    S, A, F = homolog_features.shape
    H = couple_logit_matrix.shape[1]
    D = F // H
    scale = D ** (-0.5)
    I, J, C = couple_features.shape
    per = C // R
    tokens = symbol_lookup_matrix.shape[0]

    pair_norm = normalize(couple_features).astype(bf16).reshape(I * J, C)
    projected = dot(trimul_entry_matrix[:, : 4 * C], pair_norm, ((0,), (1,)))
    bias_own = dot(couple_logit_matrix, pair_norm, ((0,), (1,)))
    valid_res = amino_present.astype(f32)
    row_valid = lax.dynamic_slice_in_dim(valid_res, lax.axis_index("res") * I, I)
    col_valid = lax.dynamic_slice_in_dim(valid_res, lax.axis_index(("br", "aux")) * J, J)
    pair_valid = (row_valid[:, None] * col_valid[None, :]).reshape(1, I * J)
    left_own = (jax.nn.sigmoid(projected[C : 2 * C]) * projected[:C] * pair_valid).astype(bf16)
    right_own = (jax.nn.sigmoid(projected[3 * C :]) * projected[2 * C : 3 * C] * pair_valid).astype(bf16)
    out_gate = jax.nn.sigmoid(dot(pair_norm, trimul_entry_matrix[:, 4 * C :], ((1,), (0,))))

    indicator = (symbol_ids.reshape(-1, 1) == jnp.arange(tokens, dtype=jnp.int32)[None, :]).astype(bf16)
    embedded = homolog_features.astype(f32).reshape(S * A, F) + dot(indicator, symbol_lookup_matrix, ((1,), (0,)))
    normed_first = normalize(embedded).astype(bf16)
    present = entry_present.astype(f32)

    rows_all, row_present, bias_all, col_present, left_all, right_all = call(
        functools.partial(first_kernel, sizes),
        "first_exchange",
        1,
        [
            ((R, S * A, F), bf16),
            ((R, S, A), f32),
            ((BR, AX, H, I * J), f32),
            ((BR, AX, S, A), f32),
            ((BR, AX, R, per, I * J), bf16),
            ((R, per, I * J), bf16),
        ],
        [(4, R), (4, R), (2, B), (2, B), (R, AX), (R, AX), (R, AX, BR), (R, AX, BR)],
        (normed_first, present, bias_own, left_own.reshape(R, per, I * J), right_own.reshape(R, per, I * J)),
    )

    row_query_gate = dot(
        normed_first,
        jnp.concatenate([horizontal_entry_matrix[:, :F], horizontal_entry_matrix[:, 3 * F :]], axis=1),
        ((1,), (0,)),
    )
    queries = row_query_gate[:, :F].astype(bf16).reshape(S, A, H, D)
    gate = jax.nn.sigmoid(row_query_gate[:, F:])
    rows = rows_all.reshape(R, S, A, F).transpose(1, 0, 2, 3).reshape(S * R * A, F)
    key_value = dot(rows, horizontal_entry_matrix[:, F : 3 * F], ((1,), (0,))).astype(bf16)
    keys = key_value[:, :F].reshape(S, R * A, H, D)
    values = key_value[:, F:].reshape(S, R * A, H, D)
    bias = bias_all.reshape(B, H, I, J).transpose(1, 2, 0, 3).reshape(H, I, B * J)
    penalty = masked_fill_value * (row_present.transpose(1, 0, 2).reshape(S, R * A) - 1.0)
    mixed = attention_row(queries, keys, values, bias, penalty, scale)
    row_mix = (gate * mixed.reshape(S * A, F)).astype(bf16)
    after_row = embedded + dot(row_mix, horizontal_exit_matrix, ((1,), (0,)))
    normed_second = normalize(after_row).astype(bf16)
    column = dot(normed_second, vertical_entry_matrix, ((1,), (0,)))
    col_keys = column[:, F : 3 * F].astype(bf16)

    product = jnp.einsum(
        "brcki,rckj->cbij",
        left_all.reshape(B, R, per, I, J),
        right_all.reshape(R, per, I, J),
        preferred_element_type=f32,
    ).astype(bf16)
    product = product.reshape(per, R, I * J).transpose(1, 0, 2)

    keys_all, product_all = call(
        functools.partial(second_kernel, sizes),
        "second_exchange",
        2,
        [((BR, AX, S * A, 2 * F), bf16), ((R, per, I * J), bf16)],
        [(R,), (R,), (AX,), (AX,), (AX, BR), (AX, BR)],
        (col_keys, product),
    )

    queries = column[:, :F].astype(bf16).reshape(S, A, H, D)
    gate = jax.nn.sigmoid(column[:, 3 * F :])
    keys = keys_all[..., :F].reshape(B * S, A, H, D)
    values = keys_all[..., F:].reshape(B * S, A, H, D)
    penalty = masked_fill_value * (col_present.reshape(B * S, A) - 1.0)
    mixed = attention_column(queries, keys, values, penalty, scale)
    col_mix = (gate * mixed.reshape(S * A, F)).astype(bf16)
    after_col = after_row + dot(col_mix, vertical_exit_matrix, ((1,), (0,)))
    normed_third = normalize(after_col).astype(bf16)
    hidden = jax.nn.relu(dot(normed_third, feedforward_first_matrix, ((1,), (0,)))).astype(bf16)
    alignment_output = (after_col + dot(hidden, feedforward_second_matrix, ((1,), (0,)))).astype(bf16)

    normed_final = normalize(product_all.reshape(C, I * J), axis=0).astype(bf16)
    update = out_gate * dot(normed_final, trimul_exit_matrix, ((0,), (0,)))
    pair_output = (couple_features.astype(f32) + update.reshape(I, J, C)).astype(bf16)
    return (alignment_output.reshape(S, A, F), pair_output)


def solution(mesh):
    sizes = (mesh.shape["res"], mesh.shape["br"], mesh.shape["aux"])
    return jax.shard_map(
        functools.partial(on_device, sizes),
        mesh=mesh,
        in_specs=(
            P(("grp", "br", "aux"), "res", None),
            P(("grp", "res"), ("br", "aux"), None),
            P(("grp", "br", "aux"), "res"),
            P(("grp", "br", "aux"), "res"),
            P("grp"),
        )
        + (P(),) * 10,
        out_specs=(P(("grp", "br", "aux"), "res", None), P(("grp", "res"), ("br", "aux"), None)),
        check_vma=False,
    )
```

```python
import functools

import jax
import jax.numpy as jnp
from jax import lax
from jax.experimental import pallas as pl
from jax.experimental.pallas import tpu as pltpu
from jax.sharding import PartitionSpec as P

epsilon = 1e-05
masked_fill_value = 1000000000.0
MESH = pl.DeviceIdType.MESH
f32 = jnp.float32
bf16 = jnp.bfloat16


def normalize(inputs, axis=-1):
    values = inputs.astype(f32)
    average = jnp.mean(values, axis=axis, keepdims=True)
    centred = values - average
    variance = jnp.mean(centred * centred, axis=axis, keepdims=True)
    return centred * lax.rsqrt(variance + epsilon)


def dot(a, b, contract):
    return lax.dot_general(a, b, (contract, ((), ())), preferred_element_type=f32)


class Peers:
    def __init__(self, sizes):
        self.R, self.BR, self.AX = sizes
        self.r = lax.axis_index("res")
        self.b = lax.axis_index("br")
        self.x = lax.axis_index("aux")

    def res(self, d):
        return lax.rem(self.r + d, self.R)

    def br(self, d):
        return lax.rem(self.b + d, self.BR)

    def aux(self, d):
        return lax.rem(self.x + d, self.AX)

    def res_back(self, d):
        return lax.rem(self.r + self.R - d, self.R)

    def aux_back(self, d):
        return lax.rem(self.x + self.AX - d, self.AX)

    def group(self):
        return [(bo, a) for bo in range(self.BR) for a in range(self.AX) if (bo, a) != (0, 0)]

    def greet(self):
        semaphore = pltpu.get_barrier_semaphore()
        for d in range(1, self.R):
            pl.semaphore_signal(semaphore, inc=1, device_id={"res": self.res(d)}, device_id_type=MESH)
        for bo, a in self.group():
            pl.semaphore_signal(
                semaphore, inc=1, device_id={"br": self.br(bo), "aux": self.aux(a)}, device_id_type=MESH
            )

    def met(self):
        pl.semaphore_wait(pltpu.get_barrier_semaphore(), self.R - 1 + self.BR * self.AX - 1)


def remote(src, dst, send, recv, device):
    copy = pltpu.make_async_remote_copy(
        src_ref=src, dst_ref=dst, send_sem=send, recv_sem=recv, device_id=device, device_id_type=MESH
    )
    copy.start()
    return copy


def iota(shape, axis):
    return lax.broadcasted_iota(jnp.int32, shape, axis)


def by_head(rows, heads):
    n, width = rows.shape
    mask = (iota((heads, width), 1) // (width // heads) == iota((heads, width), 0)).astype(f32)
    return (rows[:, None, :] * mask[None]).reshape(n * heads, width)


def from_head(rows, heads):
    n, width = rows.shape
    mask = (iota((heads, width), 1) // (width // heads) == iota((heads, width), 0)).astype(f32)
    return jnp.sum(rows.reshape(n // heads, heads, width) * mask[None], axis=1)


def attend(scores, values, heads):
    powers = jnp.exp(scores - jnp.max(scores, axis=-1, keepdims=True))
    total = jnp.sum(powers, axis=-1, keepdims=True)
    mixed = dot(powers.astype(bf16), values, ((1,), (0,)))
    return from_head(mixed / total, heads)


def joined(pieces, lanes):
    per_tile = 128 // lanes
    tiles = []
    for first in range(0, len(pieces), per_tile):
        tile = pieces[first]
        group = iota(tile.shape, 1) // lanes
        for k in range(1, min(per_tile, len(pieces) - first)):
            tile = jnp.where(group == k, pieces[first + k], tile)
        tiles.append(tile)
    return tiles[0] if len(tiles) == 1 else jnp.concatenate(tiles, axis=1)


def block_kernel(
    sizes, dims,
    homolog, couple, indicator, present, pair_valid, table, row_in, pair_in, row_exit, col_in, col_exit,
    feed_first, feed_second, gate_in, tri_exit,
    alignment, pair,
    rows_own, bias_own, left_own, right_own, keys_own, product_own,
    rows_all, row_present, bias_all, col_present, left_all, right_all, keys_all, product_all,
    embedded_s, pair_norm_s, gate_s, bias_s, key_value_s, left_s, right_s, product_s, update_s, context_s,
    res_send, res_recv, grp_send, grp_recv, aux_send, aux_recv, br_send, br_recv,
    across_send, across_recv, over_send, over_recv,
):
    p = Peers(sizes)
    R, BR, AX = sizes
    B = BR * AX
    S, A, F, H, I, J, C, per, T, N = dims
    scale = (F // H) ** (-0.5)
    Q = 128 // J
    M = J // Q
    p.greet()
    sent = []
    arriving = {"rows": [], "bias": [], "right": [], "left": [], "keys": [], "product": []}

    pair_norm = normalize(couple[...]).astype(bf16)
    pair_norm_s[...] = pair_norm
    for side, own in ((0, left_own), (1, right_own)):
        first = 2 * side * C
        value = dot(pair_in[first : first + C, :], pair_norm, ((1,), (1,)))
        sigma = jax.nn.sigmoid(dot(pair_in[first + C : first + 2 * C, :], pair_norm, ((1,), (1,))))
        value = sigma * value * pair_valid[...]
        for n in range(R):
            for t in range(T):
                own[n, t] = value[n * per : (n + 1) * per, t * 128 : (t + 1) * 128].astype(bf16)
    bias_own[...] = dot(pair_in[4 * C :, :], pair_norm, ((1,), (1,)))
    embedded = homolog[...].astype(f32) + dot(indicator[...], table[...], ((1,), (0,)))
    embedded_s[...] = embedded
    normed_first = normalize(embedded).astype(bf16)
    rows_own[...] = normed_first

    p.met()

    def relay(d, a):
        origin = (p.b, p.aux_back(a), p.res_back(d))
        src = left_own.at[p.r] if (d, a) == (0, 0) else left_all.at[origin]
        for bo in range(1, BR):
            copy = remote(
                src, left_all.at[origin], br_send.at[d, a, bo], br_recv.at[d, a, bo], {"br": p.br(bo)}
            )
            sent.append(copy)
            arriving["left"].append(copy)

    def spread(d):
        origin = (p.b, p.x, p.res_back(d))
        src = left_own.at[p.r] if d == 0 else left_all.at[origin]
        copies = {}
        for a in range(1, AX):
            copies[a] = remote(
                src, left_all.at[origin], aux_send.at[d, a], aux_recv.at[d, a], {"aux": p.aux(a)}
            )
            sent.append(copies[a])
        relay(d, 0)
        return copies

    def to_res(index, kind, pairs):
        for d in range(1, R):
            for n, (src, dst) in enumerate(pairs(p.res(d))):
                copy = remote(
                    src, dst, res_send.at[index + n, d], res_recv.at[index + n, d], {"res": p.res(d)}
                )
                sent.append(copy)
                arriving[kind].append(copy)

    lefts = {}
    for d in range(1, R):
        lefts[d] = remote(
            left_own.at[p.res(d)], left_all.at[p.b, p.x, p.r], res_send.at[0, d], res_recv.at[0, d],
            {"res": p.res(d)},
        )
        sent.append(lefts[d])
    spreads = {0: spread(0)}
    to_res(1, "rows", lambda to: ((rows_own, rows_all.at[p.r]), (present.at[0], row_present.at[p.r])))
    for n, (bo, a) in enumerate(p.group()):
        to = {"br": p.br(bo), "aux": p.aux(a)}
        for m, (src, dst) in enumerate(((bias_own, bias_all), (present.at[1], col_present))):
            copy = remote(src, dst.at[p.b, p.x], grp_send.at[m, n], grp_recv.at[m, n], to)
            sent.append(copy)
            arriving["bias"].append(copy)
    to_res(3, "right", lambda to: ((right_own.at[to], right_all.at[p.r]),))
    rows_all[p.r] = rows_own[...]
    row_present[p.r] = present[0]
    bias_all[p.b, p.x] = bias_own[...]
    col_present[p.b, p.x] = present[1]
    left_all[p.b, p.x, p.r] = left_own[p.r]
    right_all[p.r] = right_own[p.r]

    query = dot(normed_first, row_in[:, :F], ((1,), (0,))).astype(bf16).astype(f32)
    row_gate = jax.nn.sigmoid(dot(normed_first, row_in[:, 3 * F :], ((1,), (0,))))
    gate_s[...] = jax.nn.sigmoid(dot(pair_norm, gate_in[...], ((1,), (0,))))

    for d in range(1, R):
        lefts[d].wait_recv()
        spreads[d] = spread(d)
    for copy in arriving["bias"]:
        copy.wait_recv()
    for t in range(T):
        for q in range(Q):
            pieces = []
            for b in range(B):
                tile = bias_all[b // AX, b % AX, :, t * 128 : (t + 1) * 128]
                turn = (b - q) % Q * J
                pieces.append(pltpu.roll(tile, turn, 1) if turn else tile)
            row = (t * Q + q) * H
            bias_s[row : row + H, :] = joined(pieces, J)
    for d in range(R):
        for a in range(1, AX):
            spreads[d][a].wait_recv()
            relay(d, a)

    for copy in arriving["rows"]:
        copy.wait_recv()
    key_value_s[...] = (
        dot(rows_all[...].reshape(R * S * A, F), row_in[:, F : 3 * F], ((1,), (0,)))
        .astype(bf16)
        .reshape(R, S * A, 2 * F)
    )
    presence = joined([row_present[n] for n in range(R)], A)
    for s in range(S):
        mine = slice(s * A, (s + 1) * A)
        keys = key_value_s[:, mine, :F].reshape(R * A, F)
        values = key_value_s[:, mine, F:].reshape(R * A, F)
        scores = dot(by_head(query[mine], H).astype(bf16), keys, ((1,), (1,))) * scale
        scores = scores + bias_s[...] + masked_fill_value * (presence[s : s + 1] - 1.0)
        context_s[mine, :] = attend(scores, values, H)
    row_mix = (row_gate * context_s[...]).astype(bf16)
    after_row = embedded_s[...] + dot(row_mix, row_exit[...], ((1,), (0,)))
    normed_second = normalize(after_row).astype(bf16)
    keys_own[...] = dot(normed_second, col_in[:, F : 3 * F], ((1,), (0,))).astype(bf16).reshape(S, A, 2 * F)
    query = dot(normed_second, col_in[:, :F], ((1,), (0,))).astype(bf16).astype(f32)
    col_gate = jax.nn.sigmoid(dot(normed_second, col_in[:, 3 * F :], ((1,), (0,))))

    def pass_on(a):
        origin = (p.b, p.aux_back(a))
        src = keys_own if a == 0 else keys_all.at[origin]
        for bo in range(1, BR):
            copy = remote(src, keys_all.at[origin], over_send.at[a, bo], over_recv.at[a, bo], {"br": p.br(bo)})
            sent.append(copy)
            arriving["keys"].append(copy)

    across = {}
    for a in range(1, AX):
        across[a] = remote(
            keys_own, keys_all.at[p.b, p.x], across_send.at[a], across_recv.at[a], {"aux": p.aux(a)}
        )
        sent.append(across[a])
    pass_on(0)
    keys_all[p.b, p.x] = keys_own[...]

    for copy in arriving["right"]:
        copy.wait_recv()
    right_s[...] = right_all[...].astype(f32).reshape(R * T * per, 128)
    for copy in arriving["left"]:
        copy.wait_recv()
    for b in range(B):
        left_s[b] = left_all[b // AX, b % AX].astype(f32).reshape(R * T * per, 128)
    same = iota((128, 128), 0) // J == iota((128, 128), 1) // J
    group = iota((M, 128), 1) // J

    def channel(c, carry):
        pick = pl.ds(c, R * T, stride=per)
        right = jnp.transpose(right_s[pick, :]).astype(bf16)
        for b in range(B):
            grid = dot(right, left_s[b, pick, :].astype(bf16), ((1,), (0,)))
            grid = jnp.where(same, grid, 0.0)
            folded = grid[:J]
            for q in range(1, Q):
                folded = folded + grid[q * J : (q + 1) * J]
            turn = 64
            while turn >= J:
                folded = folded + pltpu.roll(folded, turn, 1)
                turn //= 2
            packed = folded[:M]
            for g in range(1, Q):
                packed = jnp.where(group == g, folded[g * M : (g + 1) * M], packed)
            product_s[b, pl.ds(pl.multiple_of(c * M, M), M), :] = packed
        return carry

    lax.fori_loop(0, per, channel, 0)
    product_own[...] = product_s[...].astype(bf16)
    for a in range(1, AX):
        across[a].wait_recv()
        pass_on(a)
    to_res(4, "product", lambda to: ((product_own.at[to], product_all.at[p.r]),))
    product_all[p.r] = product_own[p.r]

    for copy in arriving["keys"]:
        copy.wait_recv()
    presence = joined([col_present[b // AX, b % AX] for b in range(B)], S * N)
    for g in range(A // N):
        keys = keys_all[:, :, :, g * N : (g + 1) * N, :F].reshape(B * S * N, F)
        values = keys_all[:, :, :, g * N : (g + 1) * N, F:].reshape(B * S * N, F)
        rows = jnp.concatenate([query[s * A + g * N : s * A + (g + 1) * N] for s in range(S)], axis=0)
        scores = dot(by_head(rows, H).astype(bf16), keys, ((1,), (1,))) * scale
        scores = scores + masked_fill_value * (presence[g : g + 1] - 1.0)
        scores = jnp.where(iota(scores.shape, 0) // H % N == iota(scores.shape, 1) % N, scores, -1e30)
        context = attend(scores, values, H)
        for s in range(S):
            context_s[s * A + g * N : s * A + (g + 1) * N, :] = context[s * N : (s + 1) * N]
    col_mix = (col_gate * context_s[...]).astype(bf16)
    after_col = after_row + dot(col_mix, col_exit[...], ((1,), (0,)))
    normed_third = normalize(after_col).astype(bf16)
    hidden = jnp.maximum(dot(normed_third, feed_first[...], ((1,), (0,))), 0.0).astype(bf16)
    alignment[...] = (after_col + dot(hidden, feed_second[...], ((1,), (0,)))).astype(bf16)

    for copy in arriving["product"]:
        copy.wait_recv()
    normed = normalize(product_all[...].astype(f32).reshape(C, M, 128), axis=0)
    final_s = left_s.at[0]
    final_s[: C * M, :] = normed.reshape(C * M, 128)
    for m in range(M):
        turned = jnp.transpose(final_s[pl.ds(m, C, stride=M), :]).astype(bf16)
        update = dot(turned, tri_exit[...], ((1,), (0,)))
        for g in range(Q):
            update_s[pl.ds(g * M + m, I, stride=J), :] = update[g * I : (g + 1) * I]
    pair[...] = (couple[...].astype(f32) + gate_s[...] * update_s[...]).astype(bf16)
    for copy in sent:
        copy.wait_send()


def on_device(
    sizes,
    homolog_features,
    couple_features,
    symbol_ids,
    entry_present,
    amino_present,
    symbol_lookup_matrix,
    horizontal_entry_matrix,
    couple_logit_matrix,
    horizontal_exit_matrix,
    vertical_entry_matrix,
    vertical_exit_matrix,
    feedforward_first_matrix,
    feedforward_second_matrix,
    trimul_entry_matrix,
    trimul_exit_matrix,
):
    R, BR, AX = sizes
    B = BR * AX
    S, A, F = homolog_features.shape
    H = couple_logit_matrix.shape[1]
    I, J, C = couple_features.shape
    per = C // R
    T = I * J // 128
    N = 16
    assert I == J and R == B and 128 % J == 0 and 128 % A == 0 and 128 % (S * N) == 0 and A % N == 0
    M = J // (128 // J)
    tokens = symbol_lookup_matrix.shape[0]
    indicator = (symbol_ids.reshape(-1, 1) == jnp.arange(tokens, dtype=jnp.int32)[None, :]).astype(bf16)
    here = entry_present.astype(f32)
    by_row = jnp.pad(jnp.tile(here, (1, 128 // A)), ((0, 8 - S), (0, 0)))
    by_col = jnp.tile(here.reshape(S, A // N, N).transpose(1, 0, 2).reshape(A // N, S * N), (1, 128 // (S * N)))
    by_col = jnp.pad(by_col, ((0, 8 - A // N), (0, 0)))
    present = jnp.stack([by_row, by_col])
    valid_res = amino_present.astype(f32)
    row_valid = lax.dynamic_slice_in_dim(valid_res, lax.axis_index("res") * I, I)
    col_valid = lax.dynamic_slice_in_dim(valid_res, lax.axis_index(("br", "aux")) * J, J)
    pair_valid = (row_valid[:, None] * col_valid[None, :]).reshape(1, I * J)
    pair_in = jnp.concatenate([trimul_entry_matrix[:, : 4 * C], couple_logit_matrix], axis=1).T
    operands = (
        homolog_features.reshape(S * A, F),
        couple_features.reshape(I * J, C),
        indicator,
        present,
        pair_valid,
        symbol_lookup_matrix,
        horizontal_entry_matrix,
        pair_in,
        horizontal_exit_matrix,
        vertical_entry_matrix,
        vertical_exit_matrix,
        feedforward_first_matrix,
        feedforward_second_matrix,
        trimul_entry_matrix[:, 4 * C :],
        trimul_exit_matrix,
    )
    vmem = pl.BlockSpec(memory_space=pltpu.VMEM)
    buffers = [
        ((S * A, F), bf16), ((H, I * J), f32), ((R, T, per, 128), bf16), ((R, T, per, 128), bf16),
        ((S, A, 2 * F), bf16), ((R, per * M, 128), bf16),
        ((R, S * A, F), bf16), ((R, 8, 128), f32), ((BR, AX, H, I * J), f32), ((BR, AX, 8, 128), f32),
        ((BR, AX, R, T, per, 128), bf16), ((R, T, per, 128), bf16), ((BR, AX, S, A, 2 * F), bf16),
        ((R, per * M, 128), bf16),
        ((S * A, F), f32), ((I * J, C), bf16), ((I * J, C), f32), ((I * H, B * J), f32),
        ((R, S * A, 2 * F), bf16), ((B, R * T * per, 128), f32), ((R * T * per, 128), f32),
        ((R, per * M, 128), f32), ((I * J, C), f32), ((S * A, F), f32),
    ]
    semaphores = [
        (5, R), (5, R), (2, B), (2, B), (R, AX), (R, AX), (R, AX, BR), (R, AX, BR),
        (AX,), (AX,), (AX, BR), (AX, BR),
    ]
    alignment, pair = pl.pallas_call(
        functools.partial(block_kernel, sizes, (S, A, F, H, I, J, C, per, T, N)),
        name="block",
        out_shape=[jax.ShapeDtypeStruct((S * A, F), bf16), jax.ShapeDtypeStruct((I * J, C), bf16)],
        in_specs=[vmem] * len(operands),
        out_specs=[vmem] * 2,
        scratch_shapes=[pltpu.VMEM(*b) for b in buffers] + [pltpu.SemaphoreType.DMA(s) for s in semaphores],
        compiler_params=pltpu.CompilerParams(
            collective_id=1, has_side_effects=True, vmem_limit_bytes=60 * 1024 * 1024
        ),
    )(*operands)
    return (alignment.reshape(S, A, F), pair.reshape(I, J, C))


def solution(mesh):
    sizes = (mesh.shape["res"], mesh.shape["br"], mesh.shape["aux"])
    return jax.shard_map(
        functools.partial(on_device, sizes),
        mesh=mesh,
        in_specs=(
            P(("grp", "br", "aux"), "res", None),
            P(("grp", "res"), ("br", "aux"), None),
            P(("grp", "br", "aux"), "res"),
            P(("grp", "br", "aux"), "res"),
            P("grp"),
        )
        + (P(),) * 10,
        out_specs=(P(("grp", "br", "aux"), "res", None), P(("grp", "res"), ("br", "aux"), None)),
        check_vma=False,
    )
```

```python
import functools

import jax
import jax.numpy as jnp
from jax import lax
from jax.experimental import pallas as pl
from jax.experimental.pallas import tpu as pltpu
from jax.sharding import PartitionSpec as P

epsilon = 1e-05
masked_fill_value = 1000000000.0
MESH = pl.DeviceIdType.MESH
f32 = jnp.float32
bf16 = jnp.bfloat16


def normalize(inputs, axis=-1):
    values = inputs.astype(f32)
    average = jnp.mean(values, axis=axis, keepdims=True)
    centred = values - average
    variance = jnp.mean(centred * centred, axis=axis, keepdims=True)
    return centred * lax.rsqrt(variance + epsilon)


def dot(a, b, contract):
    return lax.dot_general(a, b, (contract, ((), ())), preferred_element_type=f32)


class Peers:
    def __init__(self, sizes):
        self.R, self.BR, self.AX = sizes
        self.r = lax.axis_index("res")
        self.b = lax.axis_index("br")
        self.x = lax.axis_index("aux")

    def res(self, d):
        return lax.rem(self.r + d, self.R)

    def br(self, d):
        return lax.rem(self.b + d, self.BR)

    def aux(self, d):
        return lax.rem(self.x + d, self.AX)

    def res_back(self, d):
        return lax.rem(self.r + self.R - d, self.R)

    def aux_back(self, d):
        return lax.rem(self.x + self.AX - d, self.AX)

    def group(self):
        return [(bo, a) for bo in range(self.BR) for a in range(self.AX) if (bo, a) != (0, 0)]

    def greet(self):
        semaphore = pltpu.get_barrier_semaphore()
        for d in range(1, self.R):
            pl.semaphore_signal(semaphore, inc=1, device_id={"res": self.res(d)}, device_id_type=MESH)
        for bo, a in self.group():
            pl.semaphore_signal(
                semaphore, inc=1, device_id={"br": self.br(bo), "aux": self.aux(a)}, device_id_type=MESH
            )

    def met(self):
        pl.semaphore_wait(pltpu.get_barrier_semaphore(), self.R - 1 + self.BR * self.AX - 1)


def remote(src, dst, send, recv, device):
    copy = pltpu.make_async_remote_copy(
        src_ref=src, dst_ref=dst, send_sem=send, recv_sem=recv, device_id=device, device_id_type=MESH
    )
    copy.start()
    return copy


def iota(shape, axis):
    return lax.broadcasted_iota(jnp.int32, shape, axis)


def by_head(rows, heads):
    n, width = rows.shape
    mask = (iota((heads, width), 1) // (width // heads) == iota((heads, width), 0)).astype(f32)
    return (rows[:, None, :] * mask[None]).reshape(n * heads, width)


def from_head(rows, heads):
    n, width = rows.shape
    mask = (iota((heads, width), 1) // (width // heads) == iota((heads, width), 0)).astype(f32)
    return jnp.sum(rows.reshape(n // heads, heads, width) * mask[None], axis=1)


def attend(scores, values, heads):
    powers = jnp.exp(scores - jnp.max(scores, axis=-1, keepdims=True))
    total = jnp.sum(powers, axis=-1, keepdims=True)
    mixed = dot(powers.astype(bf16), values, ((1,), (0,)))
    return from_head(mixed / total, heads)


def joined(pieces, lanes):
    per_tile = 128 // lanes
    tiles = []
    for first in range(0, len(pieces), per_tile):
        tile = pieces[first]
        group = iota(tile.shape, 1) // lanes
        for k in range(1, min(per_tile, len(pieces) - first)):
            tile = jnp.where(group == k, pieces[first + k], tile)
        tiles.append(tile)
    return tiles[0] if len(tiles) == 1 else jnp.concatenate(tiles, axis=1)


def block_kernel(
    sizes, dims,
    homolog, couple, symbols, entries, amino, table, logit, tri_in, tri_exit,
    row_in_far, row_exit_far, col_in_far, col_exit_far, feed_first_far, feed_second_far,
    alignment, pair,
    rows_own, bias_own, left_own, right_own, keys_own, product_own,
    rows_all, row_present, bias_all, col_present, left_all, right_all, keys_all, product_all,
    row_in, row_exit, col_in, col_exit, feed_first, feed_second, present,
    embedded_s, pair_norm_s, gate_s, bias_s, key_value_s, left_s, right_s, product_s, update_s, context_s,
    res_send, res_recv, grp_send, grp_recv, aux_send, aux_recv, br_send, br_recv,
    across_send, across_recv, over_send, over_recv, weight_sem,
):
    p = Peers(sizes)
    R, BR, AX = sizes
    B = BR * AX
    S, A, F, H, I, J, C, per, T, N = dims
    scale = (F // H) ** (-0.5)
    Q = 128 // J
    M = J // Q
    p.greet()
    weights = []
    for n, (far, near) in enumerate(
        (
            (row_in_far, row_in),
            (row_exit_far, row_exit),
            (col_in_far, col_in),
            (col_exit_far, col_exit),
            (feed_first_far, feed_first),
            (feed_second_far, feed_second),
        )
    ):
        weights.append(pltpu.make_async_copy(far, near, weight_sem.at[n]))
        weights[n].start()
    sent = []
    arriving = {"rows": [], "bias": [], "right": [], "left": [], "keys": [], "product": []}

    pair_norm = normalize(couple[...]).astype(bf16)
    pair_norm_s[...] = pair_norm
    alive = jnp.broadcast_to(amino[...].astype(f32), (8, amino.shape[1])).astype(bf16)
    residue = iota((amino.shape[1], I * J), 0)
    flat = iota((amino.shape[1], I * J), 1)
    row_pick = (residue == p.r * I + flat // J).astype(f32).astype(bf16)
    col_pick = (residue == (p.b * AX + p.x) * J + flat % J).astype(f32).astype(bf16)
    pair_valid = (dot(alive, row_pick, ((1,), (0,))) * dot(alive, col_pick, ((1,), (0,))))[:1]
    turned_in = [jnp.transpose(tri_in[:, n * C : (n + 1) * C].astype(f32)).astype(bf16) for n in range(4)]
    for side, own in ((0, left_own), (1, right_own)):
        value = dot(turned_in[2 * side], pair_norm, ((1,), (1,)))
        sigma = jax.nn.sigmoid(dot(turned_in[2 * side + 1], pair_norm, ((1,), (1,))))
        value = sigma * value * pair_valid
        for n in range(R):
            for t in range(T):
                own[n, t] = value[n * per : (n + 1) * per, t * 128 : (t + 1) * 128].astype(bf16)
    bias_own[...] = dot(jnp.transpose(logit[...].astype(f32)).astype(bf16), pair_norm, ((1,), (1,)))
    here = entries[...].astype(f32)
    present[...] = jnp.zeros_like(present)
    present[0, :S, :] = jnp.concatenate([here] * (128 // A), axis=1)
    for g in range(A // N):
        pieces = [here[s : s + 1, g * N : (g + 1) * N] for s in range(S)]
        present[1, g : g + 1, :] = jnp.concatenate(pieces * (128 // (S * N)), axis=1)
    tokens = table.shape[0]
    for s in range(S):
        chosen = (iota((tokens, A), 0) == symbols[s : s + 1, :]).astype(f32)
        context_s[s * A : (s + 1) * A, :] = dot(jnp.transpose(chosen).astype(bf16), table[...], ((1,), (0,)))
    embedded = homolog[...].astype(f32) + context_s[...]
    embedded_s[...] = embedded
    normed_first = normalize(embedded).astype(bf16)
    rows_own[...] = normed_first

    p.met()

    def relay(d, a):
        origin = (p.b, p.aux_back(a), p.res_back(d))
        src = left_own.at[p.r] if (d, a) == (0, 0) else left_all.at[origin]
        for bo in range(1, BR):
            copy = remote(
                src, left_all.at[origin], br_send.at[d, a, bo], br_recv.at[d, a, bo], {"br": p.br(bo)}
            )
            sent.append(copy)
            arriving["left"].append(copy)

    def spread(d):
        origin = (p.b, p.x, p.res_back(d))
        src = left_own.at[p.r] if d == 0 else left_all.at[origin]
        copies = {}
        for a in range(1, AX):
            copies[a] = remote(
                src, left_all.at[origin], aux_send.at[d, a], aux_recv.at[d, a], {"aux": p.aux(a)}
            )
            sent.append(copies[a])
        relay(d, 0)
        return copies

    def to_res(index, kind, pairs):
        for d in range(1, R):
            for n, (src, dst) in enumerate(pairs(p.res(d))):
                copy = remote(
                    src, dst, res_send.at[index + n, d], res_recv.at[index + n, d], {"res": p.res(d)}
                )
                sent.append(copy)
                arriving[kind].append(copy)

    lefts = {}
    for d in range(1, R):
        lefts[d] = remote(
            left_own.at[p.res(d)], left_all.at[p.b, p.x, p.r], res_send.at[0, d], res_recv.at[0, d],
            {"res": p.res(d)},
        )
        sent.append(lefts[d])
    spreads = {0: spread(0)}
    to_res(1, "rows", lambda to: ((rows_own, rows_all.at[p.r]), (present.at[0], row_present.at[p.r])))
    for n, (bo, a) in enumerate(p.group()):
        to = {"br": p.br(bo), "aux": p.aux(a)}
        for m, (src, dst) in enumerate(((bias_own, bias_all), (present.at[1], col_present))):
            copy = remote(src, dst.at[p.b, p.x], grp_send.at[m, n], grp_recv.at[m, n], to)
            sent.append(copy)
            arriving["bias"].append(copy)
    to_res(3, "right", lambda to: ((right_own.at[to], right_all.at[p.r]),))
    rows_all[p.r] = rows_own[...]
    row_present[p.r] = present[0]
    bias_all[p.b, p.x] = bias_own[...]
    col_present[p.b, p.x] = present[1]
    left_all[p.b, p.x, p.r] = left_own[p.r]
    right_all[p.r] = right_own[p.r]

    weights[0].wait()
    query = dot(normed_first, row_in[:, :F], ((1,), (0,))).astype(bf16).astype(f32)
    row_gate = jax.nn.sigmoid(dot(normed_first, row_in[:, 3 * F :], ((1,), (0,))))
    gate_s[...] = jax.nn.sigmoid(dot(pair_norm, tri_in[:, 4 * C :], ((1,), (0,))))

    for d in range(1, R):
        lefts[d].wait_recv()
        spreads[d] = spread(d)
    for copy in arriving["bias"]:
        copy.wait_recv()
    for t in range(T):
        for q in range(Q):
            pieces = []
            for b in range(B):
                tile = bias_all[b // AX, b % AX, :, t * 128 : (t + 1) * 128]
                turn = (b - q) % Q * J
                pieces.append(pltpu.roll(tile, turn, 1) if turn else tile)
            row = (t * Q + q) * H
            bias_s[row : row + H, :] = joined(pieces, J)
    for d in range(R):
        for a in range(1, AX):
            spreads[d][a].wait_recv()
            relay(d, a)

    for copy in arriving["rows"]:
        copy.wait_recv()
    key_value_s[...] = (
        dot(rows_all[...].reshape(R * S * A, F), row_in[:, F : 3 * F], ((1,), (0,)))
        .astype(bf16)
        .reshape(R, S * A, 2 * F)
    )
    presence = joined([row_present[n] for n in range(R)], A)
    for s in range(S):
        mine = slice(s * A, (s + 1) * A)
        keys = key_value_s[:, mine, :F].reshape(R * A, F)
        values = key_value_s[:, mine, F:].reshape(R * A, F)
        scores = dot(by_head(query[mine], H).astype(bf16), keys, ((1,), (1,))) * scale
        scores = scores + bias_s[...] + masked_fill_value * (presence[s : s + 1] - 1.0)
        context_s[mine, :] = attend(scores, values, H)
    weights[1].wait()
    weights[2].wait()
    row_mix = (row_gate * context_s[...]).astype(bf16)
    after_row = embedded_s[...] + dot(row_mix, row_exit[...], ((1,), (0,)))
    normed_second = normalize(after_row).astype(bf16)
    keys_own[...] = dot(normed_second, col_in[:, F : 3 * F], ((1,), (0,))).astype(bf16).reshape(S, A, 2 * F)
    query = dot(normed_second, col_in[:, :F], ((1,), (0,))).astype(bf16).astype(f32)
    col_gate = jax.nn.sigmoid(dot(normed_second, col_in[:, 3 * F :], ((1,), (0,))))

    def pass_on(a):
        origin = (p.b, p.aux_back(a))
        src = keys_own if a == 0 else keys_all.at[origin]
        for bo in range(1, BR):
            copy = remote(src, keys_all.at[origin], over_send.at[a, bo], over_recv.at[a, bo], {"br": p.br(bo)})
            sent.append(copy)
            arriving["keys"].append(copy)

    across = {}
    for a in range(1, AX):
        across[a] = remote(
            keys_own, keys_all.at[p.b, p.x], across_send.at[a], across_recv.at[a], {"aux": p.aux(a)}
        )
        sent.append(across[a])
    pass_on(0)
    keys_all[p.b, p.x] = keys_own[...]

    for copy in arriving["right"]:
        copy.wait_recv()
    right_s[...] = right_all[...].astype(f32).reshape(R * T * per, 128)
    for copy in arriving["left"]:
        copy.wait_recv()
    for b in range(B):
        left_s[b] = left_all[b // AX, b % AX].astype(f32).reshape(R * T * per, 128)
    wide = iota((J, 128), 1) // J
    lane = iota((M, 128), 1)

    def channel(c, carry):
        pick = pl.ds(c, R * T, stride=per)
        right = jnp.transpose(right_s[pick, :]).astype(bf16)
        lefts = jnp.concatenate([left_s[b, pick, :].astype(bf16) for b in range(B)], axis=1)
        grid = dot(right, lefts, ((1,), (0,)))
        for b in range(B):
            tile = grid[:, b * 128 : (b + 1) * 128]
            folded = tile[:J]
            for q in range(1, Q):
                folded = jnp.where(wide == q, tile[q * J : (q + 1) * J], folded)
            pieces = [folded[g * M : (g + 1) * M] for g in range(Q)]
            turn = J
            while turn < 128:
                low = (lane & turn) == 0
                pieces = [
                    jnp.where(low, pieces[k], pieces[k + 1])
                    + pltpu.roll(jnp.where(low, pieces[k + 1], pieces[k]), turn, 1)
                    for k in range(0, len(pieces), 2)
                ]
                turn *= 2
            product_s[b, pl.ds(pl.multiple_of(c * M, M), M), :] = pieces[0]
        return carry

    lax.fori_loop(0, per, channel, 0, unroll=4)
    product_own[...] = product_s[...].astype(bf16)
    for a in range(1, AX):
        across[a].wait_recv()
        pass_on(a)
    to_res(4, "product", lambda to: ((product_own.at[to], product_all.at[p.r]),))
    product_all[p.r] = product_own[p.r]

    for copy in arriving["keys"]:
        copy.wait_recv()
    presence = joined([col_present[b // AX, b % AX] for b in range(B)], S * N)
    for g in range(A // N):
        keys = keys_all[:, :, :, g * N : (g + 1) * N, :F].reshape(B * S * N, F)
        values = keys_all[:, :, :, g * N : (g + 1) * N, F:].reshape(B * S * N, F)
        rows = jnp.concatenate([query[s * A + g * N : s * A + (g + 1) * N] for s in range(S)], axis=0)
        scores = dot(by_head(rows, H).astype(bf16), keys, ((1,), (1,))) * scale
        scores = scores + masked_fill_value * (presence[g : g + 1] - 1.0)
        scores = jnp.where(iota(scores.shape, 0) // H % N == iota(scores.shape, 1) % N, scores, -1e30)
        context = attend(scores, values, H)
        for s in range(S):
            context_s[s * A + g * N : s * A + (g + 1) * N, :] = context[s * N : (s + 1) * N]
    for n in (3, 4, 5):
        weights[n].wait()
    col_mix = (col_gate * context_s[...]).astype(bf16)
    after_col = after_row + dot(col_mix, col_exit[...], ((1,), (0,)))
    normed_third = normalize(after_col).astype(bf16)
    hidden = jnp.maximum(dot(normed_third, feed_first[...], ((1,), (0,))), 0.0).astype(bf16)
    alignment[...] = (after_col + dot(hidden, feed_second[...], ((1,), (0,)))).astype(bf16)

    for copy in arriving["product"]:
        copy.wait_recv()
    normed = normalize(product_all[...].astype(f32).reshape(C, M, 128), axis=0)
    final_s = left_s.at[0]
    final_s[: C * M, :] = normed.reshape(C * M, 128)
    for m in range(M):
        turned = jnp.transpose(final_s[pl.ds(m, C, stride=M), :]).astype(bf16)
        update = dot(turned, tri_exit[...], ((1,), (0,)))
        for g in range(Q):
            update_s[pl.ds(g * M + m, I, stride=J), :] = update[g * I : (g + 1) * I]
    pair[...] = (couple[...].astype(f32) + gate_s[...] * update_s[...]).astype(bf16)
    for copy in sent:
        copy.wait_send()


def on_device(
    sizes,
    homolog_features,
    couple_features,
    symbol_ids,
    entry_present,
    amino_present,
    symbol_lookup_matrix,
    horizontal_entry_matrix,
    couple_logit_matrix,
    horizontal_exit_matrix,
    vertical_entry_matrix,
    vertical_exit_matrix,
    feedforward_first_matrix,
    feedforward_second_matrix,
    trimul_entry_matrix,
    trimul_exit_matrix,
):
    R, BR, AX = sizes
    B = BR * AX
    S, A, F = homolog_features.shape
    H = couple_logit_matrix.shape[1]
    I, J, C = couple_features.shape
    per = C // R
    T = I * J // 128
    N = 16
    assert I == J and R == B and 128 % J == 0 and 128 % A == 0 and 128 % (S * N) == 0 and A % N == 0
    M = J // (128 // J)
    near = (
        homolog_features.reshape(S * A, F),
        couple_features.reshape(I * J, C),
        symbol_ids,
        entry_present,
        amino_present.reshape(1, -1),
        symbol_lookup_matrix,
        couple_logit_matrix,
        trimul_entry_matrix,
        trimul_exit_matrix,
    )
    far = (
        horizontal_entry_matrix,
        horizontal_exit_matrix,
        vertical_entry_matrix,
        vertical_exit_matrix,
        feedforward_first_matrix,
        feedforward_second_matrix,
    )
    vmem = pl.BlockSpec(memory_space=pltpu.VMEM)
    buffers = [
        ((S * A, F), bf16), ((H, I * J), f32), ((R, T, per, 128), bf16), ((R, T, per, 128), bf16),
        ((S, A, 2 * F), bf16), ((R, per * M, 128), bf16),
        ((R, S * A, F), bf16), ((R, 8, 128), f32), ((BR, AX, H, I * J), f32), ((BR, AX, 8, 128), f32),
        ((BR, AX, R, T, per, 128), bf16), ((R, T, per, 128), bf16), ((BR, AX, S, A, 2 * F), bf16),
        ((R, per * M, 128), bf16),
        *[(weight.shape, bf16) for weight in far], ((2, 8, 128), f32),
        ((S * A, F), f32), ((I * J, C), bf16), ((I * J, C), f32), ((I * H, B * J), f32),
        ((R, S * A, 2 * F), bf16), ((B, R * T * per, 128), f32), ((R * T * per, 128), f32),
        ((R, per * M, 128), f32), ((I * J, C), f32), ((S * A, F), f32),
    ]
    semaphores = [
        (5, R), (5, R), (2, B), (2, B), (R, AX), (R, AX), (R, AX, BR), (R, AX, BR),
        (AX,), (AX,), (AX, BR), (AX, BR), (len(far),),
    ]
    alignment, pair = pl.pallas_call(
        functools.partial(block_kernel, sizes, (S, A, F, H, I, J, C, per, T, N)),
        name="block",
        out_shape=[jax.ShapeDtypeStruct((S * A, F), bf16), jax.ShapeDtypeStruct((I * J, C), bf16)],
        in_specs=[vmem] * len(near) + [pl.BlockSpec(memory_space=pl.ANY)] * len(far),
        out_specs=[vmem] * 2,
        scratch_shapes=[pltpu.VMEM(*b) for b in buffers] + [pltpu.SemaphoreType.DMA(s) for s in semaphores],
        compiler_params=pltpu.CompilerParams(
            collective_id=1, has_side_effects=True, vmem_limit_bytes=60 * 1024 * 1024
        ),
    )(*near, *far)
    return (alignment.reshape(S, A, F), pair.reshape(I, J, C))


def solution(mesh):
    sizes = (mesh.shape["res"], mesh.shape["br"], mesh.shape["aux"])
    return jax.shard_map(
        functools.partial(on_device, sizes),
        mesh=mesh,
        in_specs=(
            P(("grp", "br", "aux"), "res", None),
            P(("grp", "res"), ("br", "aux"), None),
            P(("grp", "br", "aux"), "res"),
            P(("grp", "br", "aux"), "res"),
            P("grp"),
        )
        + (P(),) * 10,
        out_specs=(P(("grp", "br", "aux"), "res", None), P(("grp", "res"), ("br", "aux"), None)),
        check_vma=False,
    )
```

```python
import functools

import jax
import jax.numpy as jnp
from jax import lax
from jax.experimental import pallas as pl
from jax.experimental.pallas import tpu as pltpu
from jax.sharding import PartitionSpec as P

epsilon = 1e-05
masked_fill_value = 1000000000.0
MESH = pl.DeviceIdType.MESH
f32 = jnp.float32
bf16 = jnp.bfloat16


def normalize(inputs, axis=-1):
    values = inputs.astype(f32)
    average = jnp.mean(values, axis=axis, keepdims=True)
    centred = values - average
    variance = jnp.mean(centred * centred, axis=axis, keepdims=True)
    return centred * lax.rsqrt(variance + epsilon)


def dot(a, b, contract):
    return lax.dot_general(a, b, (contract, ((), ())), preferred_element_type=f32)


class Peers:
    def __init__(self, sizes):
        self.R, self.BR, self.AX = sizes
        self.r = lax.axis_index("res")
        self.b = lax.axis_index("br")
        self.x = lax.axis_index("aux")

    def res(self, d):
        return lax.rem(self.r + d, self.R)

    def br(self, d):
        return lax.rem(self.b + d, self.BR)

    def aux(self, d):
        return lax.rem(self.x + d, self.AX)

    def res_back(self, d):
        return lax.rem(self.r + self.R - d, self.R)

    def aux_back(self, d):
        return lax.rem(self.x + self.AX - d, self.AX)

    def group(self):
        return [(bo, a) for bo in range(self.BR) for a in range(self.AX) if (bo, a) != (0, 0)]

    def greet(self):
        semaphore = pltpu.get_barrier_semaphore()
        for d in range(1, self.R):
            pl.semaphore_signal(semaphore, inc=1, device_id={"res": self.res(d)}, device_id_type=MESH)
        for bo, a in self.group():
            pl.semaphore_signal(
                semaphore, inc=1, device_id={"br": self.br(bo), "aux": self.aux(a)}, device_id_type=MESH
            )

    def met(self):
        pl.semaphore_wait(pltpu.get_barrier_semaphore(), self.R - 1 + self.BR * self.AX - 1)


def remote(src, dst, send, recv, device):
    copy = pltpu.make_async_remote_copy(
        src_ref=src, dst_ref=dst, send_sem=send, recv_sem=recv, device_id=device, device_id_type=MESH
    )
    copy.start()
    return copy


def iota(shape, axis):
    return lax.broadcasted_iota(jnp.int32, shape, axis)


def by_head(rows, heads):
    n, width = rows.shape
    mask = (iota((heads, width), 1) // (width // heads) == iota((heads, width), 0)).astype(f32)
    return (rows[:, None, :] * mask[None]).reshape(n * heads, width)


def from_head(rows, heads):
    n, width = rows.shape
    mask = (iota((heads, width), 1) // (width // heads) == iota((heads, width), 0)).astype(f32)
    return jnp.sum(rows.reshape(n // heads, heads, width) * mask[None], axis=1)


def attend(scores, values, heads):
    powers = jnp.exp(scores - jnp.max(scores, axis=-1, keepdims=True))
    total = jnp.sum(powers, axis=-1, keepdims=True)
    mixed = dot(powers.astype(bf16), values, ((1,), (0,)))
    return from_head(mixed / total, heads)


def joined(pieces, lanes):
    per_tile = 128 // lanes
    tiles = []
    for first in range(0, len(pieces), per_tile):
        tile = pieces[first]
        group = iota(tile.shape, 1) // lanes
        for k in range(1, min(per_tile, len(pieces) - first)):
            tile = jnp.where(group == k, pieces[first + k], tile)
        tiles.append(tile)
    return tiles[0] if len(tiles) == 1 else jnp.concatenate(tiles, axis=1)


def block_kernel(
    sizes, dims,
    homolog, couple, symbols, entries, amino, table, logit, tri_in, tri_exit,
    row_in_far, row_exit_far, col_in_far, col_exit_far, feed_first_far, feed_second_far,
    alignment, pair,
    rows_own, bias_own, left_own, right_own, keys_own, product_own,
    rows_all, row_present, bias_all, col_present, left_all, right_all, keys_all, product_all,
    row_in, row_exit, col_in, col_exit, feed_first, feed_second, present,
    embedded_s, pair_norm_s, gate_s, bias_s, key_value_s, left_s, right_s, product_s, update_s, context_s,
    res_send, res_recv, grp_send, grp_recv, aux_send, aux_recv, br_send, br_recv,
    across_send, across_recv, over_send, over_recv, weight_sem,
):
    p = Peers(sizes)
    R, BR, AX = sizes
    B = BR * AX
    S, A, F, H, I, J, C, per, T, N = dims
    scale = (F // H) ** (-0.5)
    Q = 128 // J
    M = J // Q
    p.greet()
    weights = []
    for n, (far, near) in enumerate(
        (
            (row_in_far, row_in),
            (row_exit_far, row_exit),
            (col_in_far, col_in),
            (col_exit_far, col_exit),
            (feed_first_far, feed_first),
            (feed_second_far, feed_second),
        )
    ):
        weights.append(pltpu.make_async_copy(far, near, weight_sem.at[n]))
        weights[n].start()
    sent = []
    arriving = {"rows": [], "bias": [], "right": [], "left": [], "keys": [], "product": []}

    pair_norm = normalize(couple[...]).astype(bf16)
    pair_norm_s[...] = pair_norm
    alive = jnp.broadcast_to(amino[...].astype(f32), (8, amino.shape[1])).astype(bf16)
    residue = iota((amino.shape[1], I * J), 0)
    flat = iota((amino.shape[1], I * J), 1)
    row_pick = (residue == p.r * I + flat // J).astype(f32).astype(bf16)
    col_pick = (residue == (p.b * AX + p.x) * J + flat % J).astype(f32).astype(bf16)
    pair_valid = (dot(alive, row_pick, ((1,), (0,))) * dot(alive, col_pick, ((1,), (0,))))[:1]
    turned_in = [jnp.transpose(tri_in[:, n * C : (n + 1) * C].astype(f32)).astype(bf16) for n in range(4)]
    def project(side, own):
        value = dot(turned_in[2 * side], pair_norm, ((1,), (1,)))
        sigma = jax.nn.sigmoid(dot(turned_in[2 * side + 1], pair_norm, ((1,), (1,))))
        value = sigma * value * pair_valid
        for n in range(R):
            for t in range(T):
                own[n, t] = value[n * per : (n + 1) * per, t * 128 : (t + 1) * 128].astype(bf16)
    project(0, left_own)
    bias_own[...] = dot(jnp.transpose(logit[...].astype(f32)).astype(bf16), pair_norm, ((1,), (1,)))
    here = entries[...].astype(f32)
    present[...] = jnp.zeros_like(present)
    present[0, :S, :] = jnp.concatenate([here] * (128 // A), axis=1)
    for g in range(A // N):
        pieces = [here[s : s + 1, g * N : (g + 1) * N] for s in range(S)]
        present[1, g : g + 1, :] = jnp.concatenate(pieces * (128 // (S * N)), axis=1)
    p.met()


    def relay(d, a):
        origin = (p.b, p.aux_back(a), p.res_back(d))
        src = left_own.at[p.r] if (d, a) == (0, 0) else left_all.at[origin]
        for bo in range(1, BR):
            copy = remote(
                src, left_all.at[origin], br_send.at[d, a, bo], br_recv.at[d, a, bo], {"br": p.br(bo)}
            )
            sent.append(copy)
            arriving["left"].append(copy)

    def spread(d):
        origin = (p.b, p.x, p.res_back(d))
        src = left_own.at[p.r] if d == 0 else left_all.at[origin]
        copies = {}
        for a in range(1, AX):
            copies[a] = remote(
                src, left_all.at[origin], aux_send.at[d, a], aux_recv.at[d, a], {"aux": p.aux(a)}
            )
            sent.append(copies[a])
        relay(d, 0)
        return copies

    def to_res(index, kind, pairs):
        for d in range(1, R):
            for n, (src, dst) in enumerate(pairs(p.res(d))):
                copy = remote(
                    src, dst, res_send.at[index + n, d], res_recv.at[index + n, d], {"res": p.res(d)}
                )
                sent.append(copy)
                arriving[kind].append(copy)

    lefts = {}
    for d in range(1, R):
        lefts[d] = remote(
            left_own.at[p.res(d)], left_all.at[p.b, p.x, p.r], res_send.at[0, d], res_recv.at[0, d],
            {"res": p.res(d)},
        )
        sent.append(lefts[d])
    spreads = {0: spread(0)}
    project(1, right_own)
    tokens = table.shape[0]
    for s in range(S):
        chosen = (iota((tokens, A), 0) == symbols[s : s + 1, :]).astype(f32)
        context_s[s * A : (s + 1) * A, :] = dot(jnp.transpose(chosen).astype(bf16), table[...], ((1,), (0,)))
    embedded = homolog[...].astype(f32) + context_s[...]
    embedded_s[...] = embedded
    normed_first = normalize(embedded).astype(bf16)
    rows_own[...] = normed_first

    to_res(3, "right", lambda to: ((right_own.at[to], right_all.at[p.r]),))
    to_res(1, "rows", lambda to: ((rows_own, rows_all.at[p.r]), (present.at[0], row_present.at[p.r])))
    for n, (bo, a) in enumerate(p.group()):
        to = {"br": p.br(bo), "aux": p.aux(a)}
        for m, (src, dst) in enumerate(((bias_own, bias_all), (present.at[1], col_present))):
            copy = remote(src, dst.at[p.b, p.x], grp_send.at[m, n], grp_recv.at[m, n], to)
            sent.append(copy)
            arriving["bias"].append(copy)
    rows_all[p.r] = rows_own[...]
    row_present[p.r] = present[0]
    bias_all[p.b, p.x] = bias_own[...]
    col_present[p.b, p.x] = present[1]
    left_all[p.b, p.x, p.r] = left_own[p.r]
    right_all[p.r] = right_own[p.r]

    weights[0].wait()
    query = dot(normed_first, row_in[:, :F], ((1,), (0,))).astype(bf16).astype(f32)
    row_gate = jax.nn.sigmoid(dot(normed_first, row_in[:, 3 * F :], ((1,), (0,))))
    gate_s[...] = jax.nn.sigmoid(dot(pair_norm, tri_in[:, 4 * C :], ((1,), (0,))))

    for d in range(1, R):
        lefts[d].wait_recv()
        spreads[d] = spread(d)
    for copy in arriving["bias"]:
        copy.wait_recv()
    for t in range(T):
        for q in range(Q):
            pieces = []
            for b in range(B):
                tile = bias_all[b // AX, b % AX, :, t * 128 : (t + 1) * 128]
                turn = (b - q) % Q * J
                pieces.append(pltpu.roll(tile, turn, 1) if turn else tile)
            row = (t * Q + q) * H
            bias_s[row : row + H, :] = joined(pieces, J)
    for d in range(R):
        for a in range(1, AX):
            spreads[d][a].wait_recv()
            relay(d, a)

    for copy in arriving["right"]:
        copy.wait_recv()
    right_s[...] = right_all[...].astype(f32).reshape(R * T * per, 128)
    for copy in arriving["left"]:
        copy.wait_recv()
    for b in range(B):
        left_s[b] = left_all[b // AX, b % AX].astype(f32).reshape(R * T * per, 128)
    wide = iota((J, 128), 1) // J
    lane = iota((M, 128), 1)

    def channel(c, carry):
        pick = pl.ds(c, R * T, stride=per)
        right = jnp.transpose(right_s[pick, :]).astype(bf16)
        lefts = jnp.concatenate([left_s[b, pick, :].astype(bf16) for b in range(B)], axis=1)
        grid = dot(right, lefts, ((1,), (0,)))
        for b in range(B):
            tile = grid[:, b * 128 : (b + 1) * 128]
            folded = tile[:J]
            for q in range(1, Q):
                folded = jnp.where(wide == q, tile[q * J : (q + 1) * J], folded)
            pieces = [folded[g * M : (g + 1) * M] for g in range(Q)]
            turn = J
            while turn < 128:
                low = (lane & turn) == 0
                pieces = [
                    jnp.where(low, pieces[k], pieces[k + 1])
                    + pltpu.roll(jnp.where(low, pieces[k + 1], pieces[k]), turn, 1)
                    for k in range(0, len(pieces), 2)
                ]
                turn *= 2
            product_s[b, pl.ds(pl.multiple_of(c * M, M), M), :] = pieces[0]
        return carry

    lax.fori_loop(0, per, channel, 0, unroll=4)
    product_own[...] = product_s[...].astype(bf16)
    to_res(4, "product", lambda to: ((product_own.at[to], product_all.at[p.r]),))
    product_all[p.r] = product_own[p.r]

    for copy in arriving["rows"]:
        copy.wait_recv()
    key_value_s[...] = (
        dot(rows_all[...].reshape(R * S * A, F), row_in[:, F : 3 * F], ((1,), (0,)))
        .astype(bf16)
        .reshape(R, S * A, 2 * F)
    )
    presence = joined([row_present[n] for n in range(R)], A)
    for s in range(S):
        mine = slice(s * A, (s + 1) * A)
        keys = key_value_s[:, mine, :F].reshape(R * A, F)
        values = key_value_s[:, mine, F:].reshape(R * A, F)
        scores = dot(by_head(query[mine], H).astype(bf16), keys, ((1,), (1,))) * scale
        scores = scores + bias_s[...] + masked_fill_value * (presence[s : s + 1] - 1.0)
        context_s[mine, :] = attend(scores, values, H)
    weights[1].wait()
    weights[2].wait()
    row_mix = (row_gate * context_s[...]).astype(bf16)
    after_row = embedded_s[...] + dot(row_mix, row_exit[...], ((1,), (0,)))
    normed_second = normalize(after_row).astype(bf16)
    keys_own[...] = dot(normed_second, col_in[:, F : 3 * F], ((1,), (0,))).astype(bf16).reshape(S, A, 2 * F)
    query = dot(normed_second, col_in[:, :F], ((1,), (0,))).astype(bf16).astype(f32)
    col_gate = jax.nn.sigmoid(dot(normed_second, col_in[:, 3 * F :], ((1,), (0,))))

    def pass_on(a):
        origin = (p.b, p.aux_back(a))
        src = keys_own if a == 0 else keys_all.at[origin]
        for bo in range(1, BR):
            copy = remote(src, keys_all.at[origin], over_send.at[a, bo], over_recv.at[a, bo], {"br": p.br(bo)})
            sent.append(copy)
            arriving["keys"].append(copy)

    across = {}
    for a in range(1, AX):
        across[a] = remote(
            keys_own, keys_all.at[p.b, p.x], across_send.at[a], across_recv.at[a], {"aux": p.aux(a)}
        )
        sent.append(across[a])
    pass_on(0)
    keys_all[p.b, p.x] = keys_own[...]

    for a in range(1, AX):
        across[a].wait_recv()
        pass_on(a)
    for copy in arriving["keys"]:
        copy.wait_recv()
    presence = joined([col_present[b // AX, b % AX] for b in range(B)], S * N)
    for g in range(A // N):
        keys = keys_all[:, :, :, g * N : (g + 1) * N, :F].reshape(B * S * N, F)
        values = keys_all[:, :, :, g * N : (g + 1) * N, F:].reshape(B * S * N, F)
        rows = jnp.concatenate([query[s * A + g * N : s * A + (g + 1) * N] for s in range(S)], axis=0)
        scores = dot(by_head(rows, H).astype(bf16), keys, ((1,), (1,))) * scale
        scores = scores + masked_fill_value * (presence[g : g + 1] - 1.0)
        scores = jnp.where(iota(scores.shape, 0) // H % N == iota(scores.shape, 1) % N, scores, -1e30)
        context = attend(scores, values, H)
        for s in range(S):
            context_s[s * A + g * N : s * A + (g + 1) * N, :] = context[s * N : (s + 1) * N]
    for n in (3, 4, 5):
        weights[n].wait()
    col_mix = (col_gate * context_s[...]).astype(bf16)
    after_col = after_row + dot(col_mix, col_exit[...], ((1,), (0,)))
    normed_third = normalize(after_col).astype(bf16)
    hidden = jnp.maximum(dot(normed_third, feed_first[...], ((1,), (0,))), 0.0).astype(bf16)
    alignment[...] = after_col + dot(hidden, feed_second[...], ((1,), (0,)))

    for copy in arriving["product"]:
        copy.wait_recv()
    normed = normalize(product_all[...].astype(f32).reshape(C, M, 128), axis=0)
    final_s = left_s.at[0]
    final_s[: C * M, :] = normed.reshape(C * M, 128)
    for m in range(M):
        turned = jnp.transpose(final_s[pl.ds(m, C, stride=M), :]).astype(bf16)
        update = dot(turned, tri_exit[...], ((1,), (0,)))
        for g in range(Q):
            update_s[pl.ds(g * M + m, I, stride=J), :] = update[g * I : (g + 1) * I]
    pair[...] = couple[...].astype(f32) + gate_s[...] * update_s[...]
    for copy in sent:
        copy.wait_send()


def on_device(
    sizes,
    homolog_features,
    couple_features,
    symbol_ids,
    entry_present,
    amino_present,
    symbol_lookup_matrix,
    horizontal_entry_matrix,
    couple_logit_matrix,
    horizontal_exit_matrix,
    vertical_entry_matrix,
    vertical_exit_matrix,
    feedforward_first_matrix,
    feedforward_second_matrix,
    trimul_entry_matrix,
    trimul_exit_matrix,
):
    R, BR, AX = sizes
    B = BR * AX
    S, A, F = homolog_features.shape
    H = couple_logit_matrix.shape[1]
    I, J, C = couple_features.shape
    per = C // R
    T = I * J // 128
    N = 16
    assert I == J and R == B and 128 % J == 0 and 128 % A == 0 and 128 % (S * N) == 0 and A % N == 0
    M = J // (128 // J)
    near = (
        homolog_features.reshape(S * A, F),
        couple_features.reshape(I * J, C),
        symbol_ids,
        entry_present,
        amino_present.reshape(1, -1),
        symbol_lookup_matrix,
        couple_logit_matrix,
        trimul_entry_matrix,
        trimul_exit_matrix,
    )
    far = (
        horizontal_entry_matrix,
        horizontal_exit_matrix,
        vertical_entry_matrix,
        vertical_exit_matrix,
        feedforward_first_matrix,
        feedforward_second_matrix,
    )
    vmem = pl.BlockSpec(memory_space=pltpu.VMEM)
    buffers = [
        ((S * A, F), bf16), ((H, I * J), f32), ((R, T, per, 128), bf16), ((R, T, per, 128), bf16),
        ((S, A, 2 * F), bf16), ((R, per * M, 128), bf16),
        ((R, S * A, F), bf16), ((R, 8, 128), f32), ((BR, AX, H, I * J), f32), ((BR, AX, 8, 128), f32),
        ((BR, AX, R, T, per, 128), bf16), ((R, T, per, 128), bf16), ((BR, AX, S, A, 2 * F), bf16),
        ((R, per * M, 128), bf16),
        *[(weight.shape, bf16) for weight in far], ((2, 8, 128), f32),
        ((S * A, F), f32), ((I * J, C), bf16), ((I * J, C), f32), ((I * H, B * J), f32),
        ((R, S * A, 2 * F), bf16), ((B, R * T * per, 128), f32), ((R * T * per, 128), f32),
        ((R, per * M, 128), f32), ((I * J, C), f32), ((S * A, F), f32),
    ]
    semaphores = [
        (5, R), (5, R), (2, B), (2, B), (R, AX), (R, AX), (R, AX, BR), (R, AX, BR),
        (AX,), (AX,), (AX, BR), (AX, BR), (len(far),),
    ]
    alignment, pair = pl.pallas_call(
        functools.partial(block_kernel, sizes, (S, A, F, H, I, J, C, per, T, N)),
        name="block",
        out_shape=[jax.ShapeDtypeStruct((S * A, F), f32), jax.ShapeDtypeStruct((I * J, C), f32)],
        in_specs=[vmem] * len(near) + [pl.BlockSpec(memory_space=pl.ANY)] * len(far),
        out_specs=[vmem] * 2,
        scratch_shapes=[pltpu.VMEM(*b) for b in buffers] + [pltpu.SemaphoreType.DMA(s) for s in semaphores],
        compiler_params=pltpu.CompilerParams(
            collective_id=1, has_side_effects=True, vmem_limit_bytes=60 * 1024 * 1024
        ),
    )(*near, *far)
    return (alignment.astype(bf16).reshape(S, A, F), pair.astype(bf16).reshape(I, J, C))


def solution(mesh):
    sizes = (mesh.shape["res"], mesh.shape["br"], mesh.shape["aux"])
    return jax.shard_map(
        functools.partial(on_device, sizes),
        mesh=mesh,
        in_specs=(
            P(("grp", "br", "aux"), "res", None),
            P(("grp", "res"), ("br", "aux"), None),
            P(("grp", "br", "aux"), "res"),
            P(("grp", "br", "aux"), "res"),
            P("grp"),
        )
        + (P(),) * 10,
        out_specs=(P(("grp", "br", "aux"), "res", None), P(("grp", "res"), ("br", "aux"), None)),
        check_vma=False,
    )
```
